32 devices in a mesh: seq: 8 (over z, x), doc: 4 (over y, core).
Axes of the slice: x: 2, y: 2, z: 4, core: 2. Of those that a mesh axis runs over, the one named last changes fastest.
Arguments:
- queries: bfloat16 [16384, 4096], P(('doc', 'seq')), parts along dimension 0, may hold values from -24 to 24
- keys: bfloat16 [16384, 4096], P(('doc', 'seq')), parts along dimension 0, may hold values from -24 to 24
- values: bfloat16 [16384, 4096], P(('doc', 'seq')), parts along dimension 0, may hold values from -6 to 6
Outputs:
- attended: bfloat16 [16384, 4096], P(('doc', 'seq')), parts along dimension 0
The draws below stay inside these ranges and needn't reach their ends.
There are 4 independent parts, one for each index of `doc`. The reference program is written for one: setup_inputs(seed, part) draws one part's arguments, and reference() takes and returns one part's arrays. A program takes and returns all parts, laid end to end along the dimension named above; each array names one. Nothing has to cross between parts.
All inputs are finite; a program needn't handle non-finite values. Where the reference program divides by a largest or mean magnitude, that divisor is 1e-20 or more.
Results may differ from the reference program's by a relative error of at most 0.04.
Values may be sent and summed in bfloat16 or wider, within the bound.
A program may use at most 192 MiB of HBM per device.

```python
import jax
import jax.numpy as jnp
from jax import lax

H = 32
DH = 128
M = 512
ITERS = 6
D = 4096
TOKENS = 4096


def structured_field(key, salt):
    segment = TOKENS // M
    means = 1.2 * jax.random.truncated_normal(jax.random.fold_in(key, salt), -4.0, 4.0, (M, D), jnp.float32)
    noise = 0.8 * jax.random.truncated_normal(jax.random.fold_in(key, salt + 40), -4.0, 4.0, (TOKENS, D), jnp.float32)
    return (jnp.repeat(means, segment, axis=0) + noise).astype(jnp.bfloat16)


def draw_queries(key, part):
    return structured_field(key, 1)


def draw_keys(key, part):
    return structured_field(key, 2)


def block_levels(own_key, shape, split, least, largest):
    gain = 1.0
    for axis_at, parts in split:
        heights = jax.random.uniform(jax.random.fold_in(jax.random.fold_in(own_key, 6), axis_at), (parts,), jnp.float32, least / len(split), largest / len(split))
        gain = gain * jnp.repeat(jnp.exp(heights), shape[axis_at] // parts).reshape((-1,) + (1,) * (len(shape) - 1 - axis_at))
    return gain


def centred(rng, dims, width, reach, pieces=(), kind=jnp.bfloat16):
    array = width * jax.random.normal(rng, dims, jnp.float32)
    if pieces:
        array = array * block_levels(rng, dims, pieces, -0.22, 0.18)
    return jnp.clip(array, -reach, reach).astype(kind)


def setup_inputs(seed: int = 0, part: int = 0) -> dict:
    seeds = jax.random.split(jax.random.key(seed), 4)
    part_keys = jax.random.split(jax.random.fold_in(seeds[3], part), 4)
    queries = draw_queries(jax.random.fold_in(jax.random.fold_in(seeds[3], part), 71), part)
    keys = draw_keys(jax.random.fold_in(jax.random.fold_in(seeds[3], part), 71), part)
    values = centred(part_keys[2], (TOKENS, D), 1.0, 6.0, ((0, 8),))
    return {"queries": queries, "keys": keys, "values": values}


def softmax_last(scores):
    top = jnp.max(scores, -1, keepdims=True)
    exponent_values = jnp.exp(scores - top)
    return exponent_values / jnp.sum(exponent_values, -1, keepdims=True)


def newton_schulz(kernel):
    precise = lax.Precision.HIGHEST
    row_most = jnp.max(jnp.sum(jnp.abs(kernel), 1))
    col_most = jnp.max(jnp.sum(jnp.abs(kernel), 0))
    inverse = kernel.T / (row_most * col_most)
    identity = jnp.eye(kernel.shape[0], dtype=jnp.float32)
    for sweep in range(ITERS):
        kernel_inv = jnp.dot(kernel, inverse, precision=precise)
        inner = jnp.dot(kernel_inv, 7.0 * identity - kernel_inv, precision=precise)
        middle = jnp.dot(kernel_inv, 15.0 * identity - inner, precision=precise)
        inverse = 0.25 * jnp.dot(inverse, 13.0 * identity - middle, precision=precise)
    return inverse


def reference(queries, keys, values):
    segment = TOKENS // M
    score_scale = DH ** -0.5
    land_q = (jnp.sum(queries.reshape(M, segment, D).astype(jnp.float32), 1) / segment).astype(jnp.bfloat16)
    land_k = (jnp.sum(keys.reshape(M, segment, D).astype(jnp.float32), 1) / segment).astype(jnp.bfloat16)

    def per_head(head):
        offset = (head * DH).astype(jnp.int32)
        head_q = lax.dynamic_slice_in_dim(queries, offset, DH, 1)
        head_k = lax.dynamic_slice_in_dim(keys, offset, DH, 1)
        head_v = lax.dynamic_slice_in_dim(values, offset, DH, 1)
        query_landmark_means = lax.dynamic_slice_in_dim(land_q, offset, DH, 1)
        key_landmark_means = lax.dynamic_slice_in_dim(land_k, offset, DH, 1)
        kernel = softmax_last(jnp.dot(query_landmark_means, key_landmark_means.T, preferred_element_type=jnp.float32) * score_scale)
        inverse = newton_schulz(kernel).astype(jnp.bfloat16)
        scores_b = jnp.dot(query_landmark_means, head_k.T, preferred_element_type=jnp.float32) * score_scale
        peak = jnp.max(scores_b, 1, keepdims=True)
        exponent_values = jnp.exp(scores_b - peak)
        totals = jnp.sum(exponent_values, 1, keepdims=True)
        weighted = jnp.dot(exponent_values.astype(jnp.bfloat16), head_v, preferred_element_type=jnp.float32)
        normalized_rows = (weighted / totals).astype(jnp.bfloat16)
        attention_product = jnp.dot(inverse, normalized_rows, preferred_element_type=jnp.float32).astype(jnp.bfloat16)
        attention_weight = softmax_last(jnp.dot(head_q, key_landmark_means.T, preferred_element_type=jnp.float32) * score_scale).astype(jnp.bfloat16)
        return jnp.dot(attention_weight, attention_product, preferred_element_type=jnp.float32).astype(jnp.bfloat16)

    results = lax.map(per_head, jnp.arange(H, dtype=jnp.int32))
    return jnp.transpose(results, (1, 0, 2)).reshape(TOKENS, D)
```

```python
import functools

import jax
import jax.numpy as jnp
from jax import lax
from jax.experimental import pallas as pl
from jax.experimental.pallas import tpu as pltpu
from jax.sharding import PartitionSpec as P

H = 32
DH = 128
M = 512
ITERS = 6
F32 = jnp.float32
BF16 = jnp.bfloat16
PAD = 16
SCALE = DH ** (-0.5)
VMEM_LIMIT = 60 * 1024 * 1024


def dot(a, b, dims):
    return lax.dot_general(a, b, (dims, ((), ())), preferred_element_type=F32)


NN = ((1,), (0,))
NT = ((1,), (1,))
TN = ((0,), (0,))


def cost(flops, nbytes, trans=0):
    return pl.CostEstimate(flops=int(flops), bytes_accessed=int(nbytes), transcendentals=int(trans))


def params(axes=1):
    return pltpu.CompilerParams(dimension_semantics=("arbitrary",) * axes, vmem_limit_bytes=VMEM_LIMIT)


def means_kernel(segment, x_ref, o_ref):
    rows, tokens = o_ref.shape[0], x_ref.shape[0]
    row = lax.broadcasted_iota(jnp.int32, (rows, tokens), 0)
    col = lax.broadcasted_iota(jnp.int32, (rows, tokens), 1)
    inside = jnp.logical_and(col >= row * segment, col < (row + 1) * segment)
    pick = jnp.where(inside, 1.0, 0.0).astype(BF16)
    o_ref[...] = (dot(pick, x_ref[...], NN) / segment).astype(BF16)


def means(x, rows):
    tokens, width = x.shape
    block = min(width, 1024)
    return pl.pallas_call(
        functools.partial(means_kernel, tokens // rows),
        grid=(width // block,),
        in_specs=[pl.BlockSpec((tokens, block), lambda i: (0, i))],
        out_specs=pl.BlockSpec((rows, block), lambda i: (0, i)),
        out_shape=jax.ShapeDtypeStruct((rows, width), BF16),
        compiler_params=params(),
        cost_estimate=cost(2 * rows * tokens * width, 2 * tokens * width),
        name="means",
    )(x)


def peaks_kernel(lq_ref, k_ref, o_ref):
    scores = dot(k_ref[...], lq_ref[...], NT) * SCALE
    o_ref[0] = jnp.max(scores, 0, keepdims=True)


def peaks(land_q, keys):
    tokens = keys.shape[0]
    return pl.pallas_call(
        peaks_kernel,
        grid=(H,),
        in_specs=[
            pl.BlockSpec((M, DH), lambda h: (0, h)),
            pl.BlockSpec((tokens, DH), lambda h: (0, h)),
        ],
        out_specs=pl.BlockSpec((1, 1, M), lambda h: (h, 0, 0)),
        out_shape=jax.ShapeDtypeStruct((H, 1, M), F32),
        compiler_params=params(),
        cost_estimate=cost(4 * H * tokens * M * DH, 4 * tokens * H * DH),
        name="peaks",
    )(land_q, keys)


def exchange_kernel(n, x_ref, o_ref, held, send_sem, recv_sem):
    me = lax.axis_index("seq")
    barrier = pltpu.get_barrier_semaphore()
    for step in range(1, n):
        pl.semaphore_signal(
            barrier, inc=1, device_id={"seq": lax.rem(me + step, n)}, device_id_type=pl.DeviceIdType.MESH
        )
    pl.semaphore_wait(barrier, n - 1)
    copies = []
    for step in range(1, n):
        copy = pltpu.make_async_remote_copy(
            src_ref=x_ref,
            dst_ref=held.at[step - 1],
            send_sem=send_sem.at[step - 1],
            recv_sem=recv_sem.at[step - 1],
            device_id={"seq": lax.rem(me + step, n)},
            device_id_type=pl.DeviceIdType.MESH,
        )
        copy.start()
        copies.append(copy)
    for copy in copies:
        copy.wait()
    best = x_ref[...]
    for step in range(1, n):
        best = jnp.maximum(best, held[step - 1])
    o_ref[...] = best


def exchange_max(x, n):
    return pl.pallas_call(
        functools.partial(exchange_kernel, n),
        in_specs=[pl.BlockSpec(memory_space=pltpu.VMEM)],
        out_specs=pl.BlockSpec(memory_space=pltpu.VMEM),
        out_shape=jax.ShapeDtypeStruct(x.shape, x.dtype),
        scratch_shapes=[
            pltpu.VMEM((n - 1,) + x.shape, x.dtype),
            pltpu.SemaphoreType.DMA((n - 1,)),
            pltpu.SemaphoreType.DMA((n - 1,)),
        ],
        compiler_params=pltpu.CompilerParams(collective_id=0, has_side_effects=True),
        name="exchange_max",
    )(x)


def weighted_kernel(lq_ref, k_ref, v_ref, peak_ref, o_ref):
    scores = dot(k_ref[...], lq_ref[...], NT) * SCALE
    expo = jnp.exp(scores - peak_ref[0])
    totals = jnp.sum(expo, 0, keepdims=True)
    o_ref[0, :DH, :] = dot(v_ref[...], expo.astype(BF16), TN).astype(BF16)
    o_ref[0, DH:, :] = jnp.broadcast_to(totals, (PAD, totals.shape[1])).astype(BF16)


def weighted_sums(land_q, keys, values, peak):
    tokens = keys.shape[0]
    return pl.pallas_call(
        weighted_kernel,
        grid=(H,),
        in_specs=[
            pl.BlockSpec((M, DH), lambda h: (0, h)),
            pl.BlockSpec((tokens, DH), lambda h: (0, h)),
            pl.BlockSpec((tokens, DH), lambda h: (0, h)),
            pl.BlockSpec((1, 1, M), lambda h: (h, 0, 0)),
        ],
        out_specs=pl.BlockSpec((1, DH + PAD, M), lambda h: (h, 0, 0)),
        out_shape=jax.ShapeDtypeStruct((H, DH + PAD, M), BF16),
        compiler_params=params(),
        cost_estimate=cost(8 * H * tokens * M * DH, 8 * tokens * H * DH, H * tokens * M),
        name="weighted",
    )(land_q, keys, values, peak)


def inverse_kernel(heads, pos_ref, lq_ref, lk_ref, o_ref, kern, z_ref):
    row = lax.broadcasted_iota(jnp.int32, (M, M), 0)
    col = lax.broadcasted_iota(jnp.int32, (M, M), 1)
    eye = row == col
    for h in range(heads):
        cols = slice(h * DH, (h + 1) * DH)
        scores = dot(lq_ref[:, cols], lk_ref[:, cols], NT) * SCALE
        expo = jnp.exp(scores - jnp.max(scores, 1, keepdims=True))
        kernel = expo / jnp.sum(expo, 1, keepdims=True)
        row_most = jnp.max(jnp.sum(kernel, 1, keepdims=True), 0, keepdims=True)
        col_most = jnp.max(jnp.sum(kernel, 0, keepdims=True), 1, keepdims=True)
        kern[h] = kernel.astype(BF16)
        z_ref[h] = kernel.T / (row_most * col_most)

    def sweep(i, carry):
        zs = [z_ref[h] for h in range(heads)]
        low = [z.astype(BF16) for z in zs]
        p = [dot(kern[h], low[h], NN) for h in range(heads)]
        pb = [x.astype(BF16) for x in p]
        q1 = [dot(pb[h], jnp.where(eye, 7.0 - p[h], -p[h]).astype(BF16), NN) for h in range(heads)]
        q2 = [dot(pb[h], jnp.where(eye, 15.0 - q1[h], -q1[h]).astype(BF16), NN) for h in range(heads)]
        for h in range(heads):
            z_ref[h] = 0.25 * dot(low[h], jnp.where(eye, 13.0 - q2[h], -q2[h]).astype(BF16), NN)
        return carry

    lax.fori_loop(0, ITERS, sweep, 0)
    for h in range(heads):
        o_ref[h] = z_ref[h].astype(BF16)


def inverses(land_q, land_k, position, owned):
    heads = 2 if owned % 2 == 0 else 1
    steps = owned // heads
    return pl.pallas_call(
        functools.partial(inverse_kernel, heads),
        grid_spec=pltpu.PrefetchScalarGridSpec(
            num_scalar_prefetch=1,
            grid=(steps,),
            in_specs=[
                pl.BlockSpec((M, heads * DH), lambda i, pos: (0, pos[0] * steps + i)),
                pl.BlockSpec((M, heads * DH), lambda i, pos: (0, pos[0] * steps + i)),
            ],
            out_specs=pl.BlockSpec((heads, M, M), lambda i, pos: (i, 0, 0)),
            scratch_shapes=[pltpu.VMEM((heads, M, M), BF16), pltpu.VMEM((heads, M, M), F32)],
        ),
        out_shape=jax.ShapeDtypeStruct((owned, M, M), BF16),
        compiler_params=params(),
        cost_estimate=cost(owned * ITERS * 8 * M * M * M, 4 * owned * M * M),
        name="inverse",
    )(position.reshape(1).astype(jnp.int32), land_q, land_k)


def product_kernel(inv_ref, w_ref, o_ref):
    w = w_ref[0].astype(F32)
    normed = (w[:DH] / w[DH : DH + 1]).astype(BF16)
    o_ref[0] = dot(inv_ref[0], normed, NT).astype(BF16)


def products(inverse, summed):
    owned = inverse.shape[0]
    return pl.pallas_call(
        product_kernel,
        grid=(owned,),
        in_specs=[
            pl.BlockSpec((1, M, M), lambda h: (h, 0, 0)),
            pl.BlockSpec((1, DH + PAD, M), lambda h: (h, 0, 0)),
        ],
        out_specs=pl.BlockSpec((1, M, DH), lambda h: (h, 0, 0)),
        out_shape=jax.ShapeDtypeStruct((owned, M, DH), BF16),
        compiler_params=params(),
        cost_estimate=cost(4 * owned * M * M * DH, 2 * owned * M * M),
        name="product",
    )(inverse, summed)


def weights_kernel(q_ref, lk_ref, o_ref):
    scores = dot(q_ref[...], lk_ref[...], NT) * SCALE
    expo = jnp.exp(scores - jnp.max(scores, 1, keepdims=True))
    o_ref[0] = (expo / jnp.sum(expo, 1, keepdims=True)).astype(BF16)


def token_weights(queries, land_k):
    tokens = queries.shape[0]
    return pl.pallas_call(
        weights_kernel,
        grid=(H,),
        in_specs=[
            pl.BlockSpec((tokens, DH), lambda h: (0, h)),
            pl.BlockSpec((M, DH), lambda h: (0, h)),
        ],
        out_specs=pl.BlockSpec((1, tokens, M), lambda h: (h, 0, 0)),
        out_shape=jax.ShapeDtypeStruct((H, tokens, M), BF16),
        compiler_params=params(),
        cost_estimate=cost(4 * H * tokens * M * DH, 2 * H * tokens * M, H * tokens * M),
        name="weights",
    )(queries, land_k)


def attend_kernel(w_ref, p_ref, o_ref):
    o_ref[...] = dot(w_ref[0], p_ref[0], NN).astype(BF16)


def attend(weights, product):
    tokens = weights.shape[1]
    return pl.pallas_call(
        attend_kernel,
        grid=(H,),
        in_specs=[
            pl.BlockSpec((1, tokens, M), lambda h: (h, 0, 0)),
            pl.BlockSpec((1, M, DH), lambda h: (h, 0, 0)),
        ],
        out_specs=pl.BlockSpec((tokens, DH), lambda h: (0, h)),
        out_shape=jax.ShapeDtypeStruct((tokens, H * DH), BF16),
        compiler_params=params(),
        cost_estimate=cost(4 * H * tokens * M * DH, 2 * H * tokens * M),
        name="attend",
    )(weights, product)


def body(queries, keys, values):
    devices = lax.axis_size("seq")
    position = lax.axis_index("seq")
    per_device = M // devices
    owned = H // devices
    local_q = means(queries, per_device)
    local_k = means(keys, per_device)
    land_q = lax.all_gather(local_q, "seq", axis=0, tiled=True)
    land_k = lax.all_gather(local_k, "seq", axis=0, tiled=True)
    peak = exchange_max(peaks(land_q, keys), devices)
    partial = weighted_sums(land_q, keys, values, peak)
    summed = lax.psum_scatter(partial, "seq", scatter_dimension=0, tiled=True)
    inverse = inverses(land_q, land_k, position, owned)
    own_product = products(inverse, summed)
    product = lax.all_gather(own_product, "seq", axis=0, tiled=True)
    weights = token_weights(queries, land_k)
    return attend(weights, product)


def solution(mesh):
    placed = (P(("doc", "seq"), None),) * 3
    return jax.shard_map(
        body, mesh=mesh, in_specs=placed, out_specs=P(("doc", "seq"), None), check_vma=False
    )
```

```python
import functools

import jax
import jax.numpy as jnp
from jax import lax
from jax.experimental import pallas as pl
from jax.experimental.pallas import tpu as pltpu
from jax.sharding import PartitionSpec as P

H = 32
DH = 128
M = 512
ITERS = 6
F32 = jnp.float32
BF16 = jnp.bfloat16
SCALE = DH ** (-0.5)
MESH = pl.DeviceIdType.MESH
VMEM_LIMIT = 60 * 1024 * 1024


def dot(a, b, dims):
    return lax.dot_general(a, b, (dims, ((), ())), preferred_element_type=F32)


NN = ((1,), (0,))
NT = ((1,), (1,))
TN = ((0,), (0,))


def cost(flops, nbytes, trans=0):
    return pl.CostEstimate(flops=int(flops), bytes_accessed=int(nbytes), transcendentals=int(trans))


def params(axes=1):
    return pltpu.CompilerParams(dimension_semantics=("arbitrary",) * axes, vmem_limit_bytes=VMEM_LIMIT)


def means_kernel(segment, x_ref, o_ref):
    rows, tokens = o_ref.shape[0], x_ref.shape[0]
    row = lax.broadcasted_iota(jnp.int32, (rows, tokens), 0)
    col = lax.broadcasted_iota(jnp.int32, (rows, tokens), 1)
    inside = jnp.logical_and(col >= row * segment, col < (row + 1) * segment)
    pick = jnp.where(inside, 1.0, 0.0).astype(BF16)
    o_ref[...] = (dot(pick, x_ref[...], NN) / segment).astype(BF16)


def means(x, rows):
    tokens, width = x.shape
    block = min(width, 1024)
    return pl.pallas_call(
        functools.partial(means_kernel, tokens // rows),
        grid=(width // block,),
        in_specs=[pl.BlockSpec((tokens, block), lambda i: (0, i))],
        out_specs=pl.BlockSpec((rows, block), lambda i: (0, i)),
        out_shape=jax.ShapeDtypeStruct((rows, width), BF16),
        compiler_params=params(),
        cost_estimate=cost(2 * rows * tokens * width, 2 * tokens * width),
        name="means",
    )(x)


def greet(n):
    me = lax.axis_index("seq")
    barrier = pltpu.get_barrier_semaphore()
    for step in range(1, n):
        pl.semaphore_signal(
            barrier, inc=1, device_id={"seq": lax.rem(me + step, n)}, device_id_type=MESH
        )
    pl.semaphore_wait(barrier, n - 1)


def hops(n):
    ring = n // 2
    far, near = ring // 2, (ring - 1) // 2
    return ring, far, near


def copies_of(n):
    ring, far, near = hops(n)
    return 2 + 2 * (ring - 1) + 2 * (ring - 1) + 1


def gather_kernel(n, count, *refs):
    xs, outs = refs[:count], refs[count : 2 * count]
    send_sem, recv_sem, local_sem = refs[2 * count :]
    me = lax.axis_index("seq")
    ring, far, near = hops(n)
    z, x = me // 2, lax.rem(me, 2)
    partner = z * 2 + (1 - x)

    def at(steps, side):
        return lax.rem(z + steps + 2 * ring, ring) * 2 + side

    rows = xs[0].shape[0]
    half = rows // 2
    greet(n)
    local = []
    for a in range(count):
        copy = pltpu.make_async_copy(
            xs[a], outs[a].at[pl.ds(pl.multiple_of(me * rows, rows), rows)], local_sem.at[a]
        )
        copy.start()
        local.append(copy)
    used = [0] * count
    started, done = [], set()

    def send(a, part, chunk, dest, own):
        index = used[a]
        used[a] += 1
        spot = outs[a].at[pl.ds(pl.multiple_of(chunk * rows + part * half, half), half)]
        copy = pltpu.make_async_remote_copy(
            src_ref=xs[a].at[pl.ds(part * half, half)] if own else spot,
            dst_ref=spot,
            send_sem=send_sem.at[a, index],
            recv_sem=recv_sem.at[a, index],
            device_id={"seq": dest},
            device_id_type=MESH,
        )
        copy.start()
        started.append(copy)
        return len(started) - 1

    def arrived(which):
        started[which].wait_recv()
        done.add(which)

    reach = {(0, 1): far, (0, -1): near, (1, 1): near, (1, -1): far}
    live = {}
    for a in range(count):
        live[a] = send(a, 0, me, partner, True)
        for part in (1, 0):
            for way in (1, -1):
                if reach[part, way] > 0:
                    live[a, part, way, 0] = send(a, part, me, at(way, x), True)
        send(a, 1, me, partner, True)
    for a in range(count):
        arrived(live[a])
        for way in (1, -1):
            if reach[0, way] > 0:
                live[a, 0, way, 1] = send(a, 0, partner, at(way, x), False)
    for step in range(1, far + 1):
        for a in range(count):
            for part in (1, 0):
                for way in (1, -1):
                    if step > reach[part, way]:
                        continue
                    for other in range(2 - part):
                        arrived(live[a, part, way, other])
                        chunk = at(-way * step, x if other == 0 else 1 - x)
                        if step < reach[part, way]:
                            live[a, part, way, other] = send(a, part, chunk, at(way, x), False)
                        if part == 1:
                            send(a, 1, chunk, partner, False)
    for which in range(len(started)):
        if which not in done:
            arrived(which)
    for copy in started:
        copy.wait_send()
    for copy in local:
        copy.wait()


def gather(arrays, n, ident):
    count = len(arrays)
    total = copies_of(n)
    return pl.pallas_call(
        functools.partial(gather_kernel, n, count),
        in_specs=[pl.BlockSpec(memory_space=pltpu.VMEM)] * count,
        out_specs=[pl.BlockSpec(memory_space=pl.ANY)] * count,
        out_shape=[jax.ShapeDtypeStruct((n * x.shape[0], x.shape[1]), x.dtype) for x in arrays],
        scratch_shapes=[
            pltpu.SemaphoreType.DMA((count, total)),
            pltpu.SemaphoreType.DMA((count, total)),
            pltpu.SemaphoreType.DMA((count,)),
        ],
        compiler_params=pltpu.CompilerParams(collective_id=ident, has_side_effects=True),
        name="gather",
    )(*arrays)


def landmark_kernel(n, owned, lq_ref, lk_ref, k_ref, v_ref, o_ref, out_w, out_s, in_w, in_s, kern, z_ref, send_sem, recv_sem):
    me = lax.axis_index("seq")
    greet(n)

    def partial_sums(head, slot, j):
        cols = pl.ds(pl.multiple_of(head * DH, DH), DH)
        scores = dot(k_ref[:, cols], lq_ref[:, cols], NT) * SCALE
        peak = jnp.max(scores, 0, keepdims=True)
        expo = jnp.exp(scores - peak)
        out_s[slot, 2 * j : 2 * j + 1, :] = peak
        out_s[slot, 2 * j + 1 : 2 * j + 2, :] = jnp.sum(expo, 0, keepdims=True)
        out_w[slot, j * DH : (j + 1) * DH, :] = dot(v_ref[:, cols], expo.astype(BF16), TN).astype(BF16)

    def copies(step):
        dest = {"seq": lax.rem(me + step, n)}
        return [
            pltpu.make_async_remote_copy(
                src_ref=src.at[step - 1],
                dst_ref=dst.at[step - 1],
                send_sem=send_sem.at[kind, step - 1],
                recv_sem=recv_sem.at[kind, step - 1],
                device_id=dest,
                device_id_type=MESH,
            )
            for kind, (src, dst) in enumerate(((out_w, in_w), (out_s, in_s)))
        ]

    def serve(step, carry):
        owner = lax.rem(me + step, n)
        for j in range(owned):
            partial_sums(owner * owned + j, step - 1, j)
        for copy in copies(step):
            copy.start()
        return carry

    lax.fori_loop(1, n, serve, 0)
    for j in range(owned):
        partial_sums(me * owned + j, n - 1, j)

    group = 2 if owned % 2 == 0 else 1
    row = lax.broadcasted_iota(jnp.int32, (M, M), 0)
    col = lax.broadcasted_iota(jnp.int32, (M, M), 1)
    eye = row == col
    for first in range(0, owned, group):
        for g in range(group):
            cols = pl.ds(pl.multiple_of((me * owned + first + g) * DH, DH), DH)
            scores = dot(lq_ref[:, cols], lk_ref[:, cols], NT) * SCALE
            expo = jnp.exp(scores - jnp.max(scores, 1, keepdims=True))
            kernel = expo / jnp.sum(expo, 1, keepdims=True)
            row_most = jnp.max(jnp.sum(kernel, 1, keepdims=True), 0, keepdims=True)
            col_most = jnp.max(jnp.sum(kernel, 0, keepdims=True), 1, keepdims=True)
            kern[g] = kernel.astype(BF16)
            z_ref[first + g] = kernel.T / (row_most * col_most)

        def sweep(i, carry):
            low = [z_ref[first + g].astype(BF16) for g in range(group)]
            p = [dot(kern[g], low[g], NN) for g in range(group)]
            pb = [v.astype(BF16) for v in p]
            q1 = [dot(pb[g], jnp.where(eye, 7.0 - p[g], -p[g]).astype(BF16), NN) for g in range(group)]
            q2 = [dot(pb[g], jnp.where(eye, 15.0 - q1[g], -q1[g]).astype(BF16), NN) for g in range(group)]
            for g in range(group):
                z_ref[first + g] = 0.25 * dot(low[g], jnp.where(eye, 13.0 - q2[g], -q2[g]).astype(BF16), NN)
            return carry

        lax.fori_loop(0, ITERS, sweep, 0)

    def collect(step, carry):
        for copy in copies(step):
            copy.wait_recv()
        for copy in copies(step):
            copy.wait_send()
        return carry

    lax.fori_loop(1, n, collect, 0)
    for j in range(owned):
        own_peak = out_s[n - 1, 2 * j : 2 * j + 1, :]

        def highest(i, best):
            return jnp.maximum(best, in_s[i, 2 * j : 2 * j + 1, :])

        peak = lax.fori_loop(0, n - 1, highest, own_peak)
        factor = jnp.exp(own_peak - peak)
        total = factor * out_s[n - 1, 2 * j + 1 : 2 * j + 2, :]
        summed = factor * out_w[n - 1, j * DH : (j + 1) * DH, :].astype(F32)

        def add(i, carry):
            total, summed = carry
            factor = jnp.exp(in_s[i, 2 * j : 2 * j + 1, :] - peak)
            total = total + factor * in_s[i, 2 * j + 1 : 2 * j + 2, :]
            summed = summed + factor * in_w[i, j * DH : (j + 1) * DH, :].astype(F32)
            return total, summed

        total, summed = lax.fori_loop(0, n - 1, add, (total, summed))
        normed = (summed / total).astype(BF16)
        o_ref[j] = dot(z_ref[j].astype(BF16), normed, NT).astype(BF16)


def landmark_products(land_q, land_k, keys, values, n):
    owned = H // n
    group = 2 if owned % 2 == 0 else 1
    return pl.pallas_call(
        functools.partial(landmark_kernel, n, owned),
        in_specs=[pl.BlockSpec(memory_space=pltpu.VMEM)] * 4,
        out_specs=pl.BlockSpec(memory_space=pltpu.VMEM),
        out_shape=jax.ShapeDtypeStruct((owned, M, DH), BF16),
        scratch_shapes=[
            pltpu.VMEM((n, owned * DH, M), BF16),
            pltpu.VMEM((n, 2 * owned, M), F32),
            pltpu.VMEM((n - 1, owned * DH, M), BF16),
            pltpu.VMEM((n - 1, 2 * owned, M), F32),
            pltpu.VMEM((group, M, M), BF16),
            pltpu.VMEM((owned, M, M), F32),
            pltpu.SemaphoreType.DMA((2, n - 1)),
            pltpu.SemaphoreType.DMA((2, n - 1)),
        ],
        compiler_params=pltpu.CompilerParams(
            collective_id=1, has_side_effects=True, vmem_limit_bytes=VMEM_LIMIT
        ),
        name="landmark_products",
    )(land_q, land_k, keys, values)


def weights_kernel(q_ref, lk_ref, o_ref):
    scores = dot(q_ref[...], lk_ref[...], NT) * SCALE
    expo = jnp.exp(scores - jnp.max(scores, 1, keepdims=True))
    o_ref[0] = (expo / jnp.sum(expo, 1, keepdims=True)).astype(BF16)


def token_weights(queries, land_k):
    tokens = queries.shape[0]
    return pl.pallas_call(
        weights_kernel,
        grid=(H,),
        in_specs=[
            pl.BlockSpec((tokens, DH), lambda h: (0, h)),
            pl.BlockSpec((M, DH), lambda h: (0, h)),
        ],
        out_specs=pl.BlockSpec((1, tokens, M), lambda h: (h, 0, 0)),
        out_shape=jax.ShapeDtypeStruct((H, tokens, M), BF16),
        compiler_params=params(),
        cost_estimate=cost(4 * H * tokens * M * DH, 2 * H * tokens * M, H * tokens * M),
        name="weights",
    )(queries, land_k)


def attend_kernel(w_ref, p_ref, o_ref):
    o_ref[...] = dot(w_ref[0], p_ref[0], NN).astype(BF16)


def attend(weights, product):
    tokens = weights.shape[1]
    return pl.pallas_call(
        attend_kernel,
        grid=(H,),
        in_specs=[
            pl.BlockSpec((1, tokens, M), lambda h: (h, 0, 0)),
            pl.BlockSpec((1, M, DH), lambda h: (h, 0, 0)),
        ],
        out_specs=pl.BlockSpec((tokens, DH), lambda h: (0, h)),
        out_shape=jax.ShapeDtypeStruct((tokens, H * DH), BF16),
        compiler_params=params(),
        cost_estimate=cost(4 * H * tokens * M * DH, 2 * H * tokens * M),
        name="attend",
    )(weights, product)


def body(queries, keys, values):
    devices = lax.axis_size("seq")
    per_device = M // devices
    local_q = means(queries, per_device)
    local_k = means(keys, per_device)
    land_q, land_k = gather((local_q, local_k), devices, 0)
    own_product = landmark_products(land_q, land_k, keys, values, devices)
    product = lax.all_gather(own_product, "seq", axis=0, tiled=True)
    weights = token_weights(queries, land_k)
    return attend(weights, product)


def solution(mesh):
    placed = (P(("doc", "seq"), None),) * 3
    return jax.shard_map(
        body, mesh=mesh, in_specs=placed, out_specs=P(("doc", "seq"), None), check_vma=False
    )
```

```python
import functools

import jax
import jax.numpy as jnp
from jax import lax
from jax.experimental import pallas as pl
from jax.experimental.pallas import tpu as pltpu
from jax.sharding import PartitionSpec as P

H = 32
DH = 128
M = 512
ITERS = 6
F32 = jnp.float32
BF16 = jnp.bfloat16
SCALE = DH ** (-0.5)
MESH = pl.DeviceIdType.MESH
VMEM_LIMIT = 60 * 1024 * 1024


def dot(a, b, dims):
    return lax.dot_general(a, b, (dims, ((), ())), preferred_element_type=F32)


NN = ((1,), (0,))
NT = ((1,), (1,))
TN = ((0,), (0,))


def cost(flops, nbytes, trans=0):
    return pl.CostEstimate(flops=int(flops), bytes_accessed=int(nbytes), transcendentals=int(trans))


def params(axes=1):
    return pltpu.CompilerParams(dimension_semantics=("arbitrary",) * axes, vmem_limit_bytes=VMEM_LIMIT)


def means_kernel(segment, x_ref, o_ref):
    rows, tokens = o_ref.shape[0], x_ref.shape[0]
    row = lax.broadcasted_iota(jnp.int32, (rows, tokens), 0)
    col = lax.broadcasted_iota(jnp.int32, (rows, tokens), 1)
    inside = jnp.logical_and(col >= row * segment, col < (row + 1) * segment)
    pick = jnp.where(inside, 1.0, 0.0).astype(BF16)
    o_ref[...] = (dot(pick, x_ref[...], NN) / segment).astype(BF16)


def means(x, rows):
    tokens, width = x.shape
    block = min(width, 1024)
    return pl.pallas_call(
        functools.partial(means_kernel, tokens // rows),
        grid=(width // block,),
        in_specs=[pl.BlockSpec((tokens, block), lambda i: (0, i))],
        out_specs=pl.BlockSpec((rows, block), lambda i: (0, i)),
        out_shape=jax.ShapeDtypeStruct((rows, width), BF16),
        compiler_params=params(),
        cost_estimate=cost(2 * rows * tokens * width, 2 * tokens * width),
        name="means",
    )(x)


def greet(n):
    me = lax.axis_index("seq")
    barrier = pltpu.get_barrier_semaphore()
    for step in range(1, n):
        pl.semaphore_signal(
            barrier, inc=1, device_id={"seq": lax.rem(me + step, n)}, device_id_type=MESH
        )
    pl.semaphore_wait(barrier, n - 1)


def hops(n):
    ring = n // 2
    far, near = ring // 2, (ring - 1) // 2
    return ring, far, near


def copies_of(n):
    ring, far, near = hops(n)
    return 2 + 2 * (ring - 1) + 2 * (ring - 1) + 1


def gather_stages(n, xs, outs, send_sem, recv_sem, local_sem):
    count = len(xs)
    me = lax.axis_index("seq")
    ring, far, near = hops(n)
    z, x = me // 2, lax.rem(me, 2)
    partner = z * 2 + (1 - x)

    def at(steps, side):
        return lax.rem(z + steps + 2 * ring, ring) * 2 + side

    rows = xs[0].shape[0]
    first = max(8, rows // 64 * 8)
    spans = ((0, first), (first, rows - first))
    greet(n)
    local = []
    for a in range(count):
        copy = pltpu.make_async_copy(
            xs[a], outs[a].at[pl.ds(pl.multiple_of(me * rows, rows), rows)], local_sem.at[a]
        )
        copy.start()
        local.append(copy)
    used = [0] * count
    started, done = [], set()

    def send(a, part, chunk, dest, own):
        index = used[a]
        used[a] += 1
        low, size = spans[part]
        spot = outs[a].at[pl.ds(pl.multiple_of(chunk * rows + low, 8), size)]
        copy = pltpu.make_async_remote_copy(
            src_ref=xs[a].at[pl.ds(low, size)] if own else spot,
            dst_ref=spot,
            send_sem=send_sem.at[a, index],
            recv_sem=recv_sem.at[a, index],
            device_id={"seq": dest},
            device_id_type=MESH,
        )
        copy.start()
        started.append(copy)
        return len(started) - 1

    def arrived(which):
        started[which].wait_recv()
        done.add(which)

    reach = {(0, 1): far, (0, -1): near, (1, 1): near, (1, -1): far}
    live = {}
    for a in range(count):
        live[a] = send(a, 0, me, partner, True)
        for part in (1, 0):
            for way in (1, -1):
                if reach[part, way] > 0:
                    live[a, part, way, 0] = send(a, part, me, at(way, x), True)
        send(a, 1, me, partner, True)
    yield
    for a in range(count):
        arrived(live[a])
        for way in (1, -1):
            if reach[0, way] > 0:
                live[a, 0, way, 1] = send(a, 0, partner, at(way, x), False)
    for step in range(1, far + 1):
        yield
        for a in range(count):
            for part in (1, 0):
                for way in (1, -1):
                    if step > reach[part, way]:
                        continue
                    for other in range(2 - part):
                        arrived(live[a, part, way, other])
                        chunk = at(-way * step, x if other == 0 else 1 - x)
                        if step < reach[part, way]:
                            live[a, part, way, other] = send(a, part, chunk, at(way, x), False)
                        if part == 1:
                            send(a, 1, chunk, partner, False)
    yield
    for which in range(len(started)):
        if which not in done:
            arrived(which)
    for copy in started:
        copy.wait_send()
    for copy in local:
        copy.wait()


def gather_kernel(n, count, *refs):
    for _ in gather_stages(n, refs[:count], refs[count : 2 * count], *refs[2 * count :]):
        pass


def gather(arrays, n, ident):
    count = len(arrays)
    total = copies_of(n)
    return pl.pallas_call(
        functools.partial(gather_kernel, n, count),
        in_specs=[pl.BlockSpec(memory_space=pltpu.VMEM)] * count,
        out_specs=[pl.BlockSpec(memory_space=pl.ANY)] * count,
        out_shape=[jax.ShapeDtypeStruct((n * x.shape[0], x.shape[1]), x.dtype) for x in arrays],
        scratch_shapes=[
            pltpu.SemaphoreType.DMA((count, total)),
            pltpu.SemaphoreType.DMA((count, total)),
            pltpu.SemaphoreType.DMA((count,)),
        ],
        compiler_params=pltpu.CompilerParams(collective_id=ident, has_side_effects=True),
        name="gather",
    )(*arrays)


def landmark_kernel(n, owned, lq_ref, lk_ref, k_ref, v_ref, o_ref, out_w, out_s, in_w, in_s, kern, z_ref, send_sem, recv_sem):
    me = lax.axis_index("seq")
    greet(n)

    def partial_sums(head, slot, j):
        cols = pl.ds(pl.multiple_of(head * DH, DH), DH)
        scores = dot(k_ref[:, cols], lq_ref[:, cols], NT) * SCALE
        peak = jnp.max(scores, 0, keepdims=True)
        expo = jnp.exp(scores - peak)
        out_s[slot, 2 * j : 2 * j + 1, :] = peak
        out_s[slot, 2 * j + 1 : 2 * j + 2, :] = jnp.sum(expo, 0, keepdims=True)
        out_w[slot, j * DH : (j + 1) * DH, :] = dot(v_ref[:, cols], expo.astype(BF16), TN).astype(BF16)

    def copies(step):
        dest = {"seq": lax.rem(me + step, n)}
        return [
            pltpu.make_async_remote_copy(
                src_ref=src.at[step - 1],
                dst_ref=dst.at[step - 1],
                send_sem=send_sem.at[kind, step - 1],
                recv_sem=recv_sem.at[kind, step - 1],
                device_id=dest,
                device_id_type=MESH,
            )
            for kind, (src, dst) in enumerate(((out_w, in_w), (out_s, in_s)))
        ]

    def serve(step, carry):
        owner = lax.rem(me + step, n)
        for j in range(owned):
            partial_sums(owner * owned + j, step - 1, j)
        for copy in copies(step):
            copy.start()
        return carry

    lax.fori_loop(1, n, serve, 0)
    for j in range(owned):
        partial_sums(me * owned + j, n - 1, j)

    group = 2 if owned % 2 == 0 else 1
    row = lax.broadcasted_iota(jnp.int32, (M, M), 0)
    col = lax.broadcasted_iota(jnp.int32, (M, M), 1)
    eye = row == col
    for first in range(0, owned, group):
        for g in range(group):
            cols = pl.ds(pl.multiple_of((me * owned + first + g) * DH, DH), DH)
            scores = dot(lq_ref[:, cols], lk_ref[:, cols], NT) * SCALE
            expo = jnp.exp(scores - jnp.max(scores, 1, keepdims=True))
            kernel = expo / jnp.sum(expo, 1, keepdims=True)
            row_most = jnp.max(jnp.sum(kernel, 1, keepdims=True), 0, keepdims=True)
            col_most = jnp.max(jnp.sum(kernel, 0, keepdims=True), 1, keepdims=True)
            kern[g] = kernel.astype(BF16)
            z_ref[first + g] = kernel.T / (row_most * col_most)

        def sweep(i, carry):
            low = [z_ref[first + g].astype(BF16) for g in range(group)]
            p = [dot(kern[g], low[g], NN) for g in range(group)]
            pb = [v.astype(BF16) for v in p]
            q1 = [dot(pb[g], jnp.where(eye, 7.0 - p[g], -p[g]).astype(BF16), NN) for g in range(group)]
            q2 = [dot(pb[g], jnp.where(eye, 15.0 - q1[g], -q1[g]).astype(BF16), NN) for g in range(group)]
            for g in range(group):
                z_ref[first + g] = 0.25 * dot(low[g], jnp.where(eye, 13.0 - q2[g], -q2[g]).astype(BF16), NN)
            return carry

        lax.fori_loop(0, ITERS, sweep, 0)

    def collect(step, carry):
        for copy in copies(step):
            copy.wait_recv()
        for copy in copies(step):
            copy.wait_send()
        return carry

    lax.fori_loop(1, n, collect, 0)
    for j in range(owned):
        own_peak = out_s[n - 1, 2 * j : 2 * j + 1, :]

        def highest(i, best):
            return jnp.maximum(best, in_s[i, 2 * j : 2 * j + 1, :])

        peak = lax.fori_loop(0, n - 1, highest, own_peak)
        factor = jnp.exp(own_peak - peak)
        total = factor * out_s[n - 1, 2 * j + 1 : 2 * j + 2, :]
        summed = factor * out_w[n - 1, j * DH : (j + 1) * DH, :].astype(F32)

        def add(i, carry):
            total, summed = carry
            factor = jnp.exp(in_s[i, 2 * j : 2 * j + 1, :] - peak)
            total = total + factor * in_s[i, 2 * j + 1 : 2 * j + 2, :]
            summed = summed + factor * in_w[i, j * DH : (j + 1) * DH, :].astype(F32)
            return total, summed

        total, summed = lax.fori_loop(0, n - 1, add, (total, summed))
        normed = (summed / total).astype(BF16)
        o_ref[j] = dot(z_ref[j].astype(BF16), normed, NT).astype(BF16)


def landmark_products(land_q, land_k, keys, values, n):
    owned = H // n
    group = 2 if owned % 2 == 0 else 1
    return pl.pallas_call(
        functools.partial(landmark_kernel, n, owned),
        in_specs=[pl.BlockSpec(memory_space=pltpu.VMEM)] * 4,
        out_specs=pl.BlockSpec(memory_space=pltpu.VMEM),
        out_shape=jax.ShapeDtypeStruct((owned, M, DH), BF16),
        scratch_shapes=[
            pltpu.VMEM((n, owned * DH, M), BF16),
            pltpu.VMEM((n, 2 * owned, M), F32),
            pltpu.VMEM((n - 1, owned * DH, M), BF16),
            pltpu.VMEM((n - 1, 2 * owned, M), F32),
            pltpu.VMEM((group, M, M), BF16),
            pltpu.VMEM((owned, M, M), F32),
            pltpu.SemaphoreType.DMA((2, n - 1)),
            pltpu.SemaphoreType.DMA((2, n - 1)),
        ],
        compiler_params=pltpu.CompilerParams(
            collective_id=1, has_side_effects=True, vmem_limit_bytes=VMEM_LIMIT
        ),
        name="landmark_products",
    )(land_q, land_k, keys, values)


def final_kernel(n, own_ref, q_ref, lk_ref, o_ref, held, weights, send_sem, recv_sem, local_sem):
    def weigh(head, carry):
        cols = pl.ds(pl.multiple_of(head * DH, DH), DH)
        scores = dot(q_ref[:, cols], lk_ref[:, cols], NT) * SCALE
        expo = jnp.exp(scores - jnp.max(scores, 1, keepdims=True))
        weights[head] = (expo / jnp.sum(expo, 1, keepdims=True)).astype(BF16)
        return carry

    pieces = hops(n)[1] + 2
    at = 0
    for piece, _ in enumerate(gather_stages(n, [own_ref], [held], send_sem, recv_sem, local_sem)):
        until = H * (piece + 1) // pieces
        lax.fori_loop(at, until, weigh, 0)
        at = until

    def attend(head, carry):
        cols = pl.ds(pl.multiple_of(head * DH, DH), DH)
        rows = pl.ds(pl.multiple_of(head * M, M), M)
        o_ref[:, cols] = dot(weights[head], held[rows, :], NN).astype(BF16)
        return carry

    lax.fori_loop(0, H, attend, 0)


def final(own_product, queries, land_k, n):
    tokens, width = queries.shape
    total = copies_of(n)
    return pl.pallas_call(
        functools.partial(final_kernel, n),
        in_specs=[pl.BlockSpec(memory_space=pltpu.VMEM)] * 3,
        out_specs=pl.BlockSpec(memory_space=pltpu.VMEM),
        out_shape=jax.ShapeDtypeStruct((tokens, width), BF16),
        scratch_shapes=[
            pltpu.VMEM((H * M, DH), BF16),
            pltpu.VMEM((H, tokens, M), BF16),
            pltpu.SemaphoreType.DMA((1, total)),
            pltpu.SemaphoreType.DMA((1, total)),
            pltpu.SemaphoreType.DMA((1,)),
        ],
        compiler_params=pltpu.CompilerParams(
            collective_id=2, has_side_effects=True, vmem_limit_bytes=VMEM_LIMIT
        ),
        name="final",
    )(own_product, queries, land_k)


def body(queries, keys, values):
    devices = lax.axis_size("seq")
    per_device = M // devices
    local_q = means(queries, per_device)
    local_k = means(keys, per_device)
    land_q, land_k = gather((local_q, local_k), devices, 0)
    own_product = landmark_products(land_q, land_k, keys, values, devices)
    return final(own_product.reshape(-1, DH), queries, land_k, devices)


def solution(mesh):
    placed = (P(("doc", "seq"), None),) * 3
    return jax.shard_map(
        body, mesh=mesh, in_specs=placed, out_specs=P(("doc", "seq"), None), check_vma=False
    )
```

```python
import functools

import jax
import jax.numpy as jnp
from jax import lax
from jax.experimental import pallas as pl
from jax.experimental.pallas import tpu as pltpu
from jax.sharding import PartitionSpec as P

H = 32
DH = 128
M = 512
ITERS = 6
F32 = jnp.float32
BF16 = jnp.bfloat16
SCALE = DH ** (-0.5)
MESH = pl.DeviceIdType.MESH
VMEM_LIMIT = 60 * 1024 * 1024


def dot(a, b, dims):
    return lax.dot_general(a, b, (dims, ((), ())), preferred_element_type=F32)


NN = ((1,), (0,))
NT = ((1,), (1,))
TN = ((0,), (0,))


def cost(flops, nbytes, trans=0):
    return pl.CostEstimate(flops=int(flops), bytes_accessed=int(nbytes), transcendentals=int(trans))


def params(axes=1):
    return pltpu.CompilerParams(dimension_semantics=("arbitrary",) * axes, vmem_limit_bytes=VMEM_LIMIT)


def means_kernel(segment, x_ref, o_ref):
    rows, tokens = o_ref.shape[0], x_ref.shape[0]
    row = lax.broadcasted_iota(jnp.int32, (rows, tokens), 0)
    col = lax.broadcasted_iota(jnp.int32, (rows, tokens), 1)
    inside = jnp.logical_and(col >= row * segment, col < (row + 1) * segment)
    pick = jnp.where(inside, 1.0, 0.0).astype(BF16)
    o_ref[...] = (dot(pick, x_ref[...], NN) / segment).astype(BF16)


def means(x, rows):
    tokens, width = x.shape
    block = min(width, 1024)
    return pl.pallas_call(
        functools.partial(means_kernel, tokens // rows),
        grid=(width // block,),
        in_specs=[pl.BlockSpec((tokens, block), lambda i: (0, i))],
        out_specs=pl.BlockSpec((rows, block), lambda i: (0, i)),
        out_shape=jax.ShapeDtypeStruct((rows, width), BF16),
        compiler_params=params(),
        cost_estimate=cost(2 * rows * tokens * width, 2 * tokens * width),
        name="means",
    )(x)


def greet(n):
    me = lax.axis_index("seq")
    barrier = pltpu.get_barrier_semaphore()
    for step in range(1, n):
        pl.semaphore_signal(
            barrier, inc=1, device_id={"seq": lax.rem(me + step, n)}, device_id_type=MESH
        )
    pl.semaphore_wait(barrier, n - 1)


def hops(n):
    ring = n // 2
    far, near = ring // 2, (ring - 1) // 2
    return ring, far, near


def copies_of(n):
    ring, far, near = hops(n)
    return 2 + 2 * (ring - 1) + 2 * (ring - 1) + 1


def gather_stages(n, xs, outs, send_sem, recv_sem, local_sem):
    count = len(xs)
    me = lax.axis_index("seq")
    ring, far, near = hops(n)
    z, x = me // 2, lax.rem(me, 2)
    partner = z * 2 + (1 - x)

    def at(steps, side):
        return lax.rem(z + steps + 2 * ring, ring) * 2 + side

    rows = xs[0].shape[0]
    first = max(8, rows // 64 * 8)
    spans = ((0, first), (first, rows - first))
    greet(n)
    local = []
    for a in range(count):
        copy = pltpu.make_async_copy(
            xs[a], outs[a].at[pl.ds(pl.multiple_of(me * rows, rows), rows)], local_sem.at[a]
        )
        copy.start()
        local.append(copy)
    used = [0] * count
    started, done = [], set()

    def send(a, part, chunk, dest, own):
        index = used[a]
        used[a] += 1
        low, size = spans[part]
        spot = outs[a].at[pl.ds(pl.multiple_of(chunk * rows + low, 8), size)]
        copy = pltpu.make_async_remote_copy(
            src_ref=xs[a].at[pl.ds(low, size)] if own else spot,
            dst_ref=spot,
            send_sem=send_sem.at[a, index],
            recv_sem=recv_sem.at[a, index],
            device_id={"seq": dest},
            device_id_type=MESH,
        )
        copy.start()
        started.append(copy)
        return len(started) - 1

    def arrived(which):
        started[which].wait_recv()
        done.add(which)

    reach = {(0, 1): far, (0, -1): near, (1, 1): near, (1, -1): far}
    live = {}
    for a in range(count):
        live[a] = send(a, 0, me, partner, True)
        for part in (1, 0):
            for way in (1, -1):
                if reach[part, way] > 0:
                    live[a, part, way, 0] = send(a, part, me, at(way, x), True)
        send(a, 1, me, partner, True)
    yield
    for a in range(count):
        arrived(live[a])
        for way in (1, -1):
            if reach[0, way] > 0:
                live[a, 0, way, 1] = send(a, 0, partner, at(way, x), False)
    for step in range(1, far + 1):
        yield
        for a in range(count):
            for part in (1, 0):
                for way in (1, -1):
                    if step > reach[part, way]:
                        continue
                    for other in range(2 - part):
                        arrived(live[a, part, way, other])
                        chunk = at(-way * step, x if other == 0 else 1 - x)
                        if step < reach[part, way]:
                            live[a, part, way, other] = send(a, part, chunk, at(way, x), False)
                        if part == 1:
                            send(a, 1, chunk, partner, False)
    yield
    for which in range(len(started)):
        if which not in done:
            arrived(which)
    for copy in started:
        copy.wait_send()
    for copy in local:
        copy.wait()


def gather_kernel(n, count, *refs):
    for _ in gather_stages(n, refs[:count], refs[count : 2 * count], *refs[2 * count :]):
        pass


def gather(arrays, n, ident):
    count = len(arrays)
    total = copies_of(n)
    return pl.pallas_call(
        functools.partial(gather_kernel, n, count),
        in_specs=[pl.BlockSpec(memory_space=pltpu.VMEM)] * count,
        out_specs=[pl.BlockSpec(memory_space=pl.ANY)] * count,
        out_shape=[jax.ShapeDtypeStruct((n * x.shape[0], x.shape[1]), x.dtype) for x in arrays],
        scratch_shapes=[
            pltpu.SemaphoreType.DMA((count, total)),
            pltpu.SemaphoreType.DMA((count, total)),
            pltpu.SemaphoreType.DMA((count,)),
        ],
        compiler_params=pltpu.CompilerParams(collective_id=ident, has_side_effects=True),
        name="gather",
    )(*arrays)


def landmark_kernel(
    n, owned, lq_ref, x_ref, k_ref, v_ref, o_ref, lk_ref, out_w, out_s, in_w, in_s, kern, z_ref, own_k,
    send_sem, recv_sem, ring_send, ring_recv, local_sem, own_sem,
):
    me = lax.axis_index("seq")

    def partial_sums(head, slot, j):
        cols = pl.ds(pl.multiple_of(head * DH, DH), DH)
        scores = dot(k_ref[:, cols], lq_ref[:, cols], NT) * SCALE
        peak = jnp.max(scores, 0, keepdims=True)
        expo = jnp.exp(scores - peak)
        out_s[slot, 2 * j : 2 * j + 1, :] = peak
        out_s[slot, 2 * j + 1 : 2 * j + 2, :] = jnp.sum(expo, 0, keepdims=True)
        out_w[slot, j * DH : (j + 1) * DH, :] = dot(v_ref[:, cols], expo.astype(BF16), TN).astype(BF16)

    def copies(step):
        dest = {"seq": lax.rem(me + step, n)}
        return [
            pltpu.make_async_remote_copy(
                src_ref=src.at[step - 1],
                dst_ref=dst.at[step - 1],
                send_sem=send_sem.at[kind, step - 1],
                recv_sem=recv_sem.at[kind, step - 1],
                device_id=dest,
                device_id_type=MESH,
            )
            for kind, (src, dst) in enumerate(((out_w, in_w), (out_s, in_s)))
        ]

    def serve(turn, carry):
        step = n // 2 + (turn + 1) // 2 * (1 - 2 * lax.rem(turn, 2))
        owner = lax.rem(me + step, n)
        for j in range(owned):
            partial_sums(owner * owned + j, step - 1, j)
        for copy in copies(step):
            copy.start()
        return carry

    pieces = hops(n)[1] + 2
    at = 0
    for piece, _ in enumerate(gather_stages(n, [x_ref], [lk_ref], ring_send, ring_recv, local_sem)):
        until = (n - 1) * (piece + 1) // pieces
        lax.fori_loop(at, until, serve, 0)
        at = until
        if piece == pieces - 1:
            for j in range(owned):
                partial_sums(me * owned + j, n - 1, j)
    own_cols = pl.ds(pl.multiple_of(me * owned * DH, DH), owned * DH)
    fetch = pltpu.make_async_copy(lk_ref.at[:, own_cols], own_k, own_sem)
    fetch.start()
    fetch.wait()

    group = 2 if owned % 2 == 0 else 1
    row = lax.broadcasted_iota(jnp.int32, (M, M), 0)
    col = lax.broadcasted_iota(jnp.int32, (M, M), 1)
    eye = row == col
    for first in range(0, owned, group):
        for g in range(group):
            cols = pl.ds(pl.multiple_of((me * owned + first + g) * DH, DH), DH)
            scores = dot(lq_ref[:, cols], own_k[:, (first + g) * DH : (first + g + 1) * DH], NT) * SCALE
            expo = jnp.exp(scores - jnp.max(scores, 1, keepdims=True))
            kernel = expo / jnp.sum(expo, 1, keepdims=True)
            row_most = jnp.max(jnp.sum(kernel, 1, keepdims=True), 0, keepdims=True)
            col_most = jnp.max(jnp.sum(kernel, 0, keepdims=True), 1, keepdims=True)
            kern[g] = kernel.astype(BF16)
            z_ref[first + g] = kernel.T / (row_most * col_most)

        def sweep(i, carry):
            low = [z_ref[first + g].astype(BF16) for g in range(group)]
            p = [dot(kern[g], low[g], NN) for g in range(group)]
            pb = [v.astype(BF16) for v in p]
            q1 = [dot(pb[g], jnp.where(eye, 7.0 - p[g], -p[g]).astype(BF16), NN) for g in range(group)]
            q2 = [dot(pb[g], jnp.where(eye, 15.0 - q1[g], -q1[g]).astype(BF16), NN) for g in range(group)]
            for g in range(group):
                z_ref[first + g] = 0.25 * dot(low[g], jnp.where(eye, 13.0 - q2[g], -q2[g]).astype(BF16), NN)
            return carry

        lax.fori_loop(0, ITERS, sweep, 0)

    def collect(step, carry):
        for copy in copies(step):
            copy.wait_recv()
        for copy in copies(step):
            copy.wait_send()
        return carry

    lax.fori_loop(1, n, collect, 0)
    for j in range(owned):
        own_peak = out_s[n - 1, 2 * j : 2 * j + 1, :]

        def highest(i, best):
            return jnp.maximum(best, in_s[i, 2 * j : 2 * j + 1, :])

        peak = lax.fori_loop(0, n - 1, highest, own_peak)
        factor = jnp.exp(own_peak - peak)
        total = factor * out_s[n - 1, 2 * j + 1 : 2 * j + 2, :]
        summed = factor * out_w[n - 1, j * DH : (j + 1) * DH, :].astype(F32)

        def add(i, carry):
            total, summed = carry
            factor = jnp.exp(in_s[i, 2 * j : 2 * j + 1, :] - peak)
            total = total + factor * in_s[i, 2 * j + 1 : 2 * j + 2, :]
            summed = summed + factor * in_w[i, j * DH : (j + 1) * DH, :].astype(F32)
            return total, summed

        total, summed = lax.fori_loop(0, n - 1, add, (total, summed))
        normed = (summed / total).astype(BF16)
        o_ref[j] = dot(z_ref[j].astype(BF16), normed, NT).astype(BF16)


def landmark_products(land_q, local_k, keys, values, n):
    owned = H // n
    group = 2 if owned % 2 == 0 else 1
    return pl.pallas_call(
        functools.partial(landmark_kernel, n, owned),
        in_specs=[pl.BlockSpec(memory_space=pltpu.VMEM)] * 4,
        out_specs=[pl.BlockSpec(memory_space=pltpu.VMEM), pl.BlockSpec(memory_space=pl.ANY)],
        out_shape=[
            jax.ShapeDtypeStruct((owned, M, DH), BF16),
            jax.ShapeDtypeStruct((n * local_k.shape[0], local_k.shape[1]), BF16),
        ],
        scratch_shapes=[
            pltpu.VMEM((n, owned * DH, M), BF16),
            pltpu.VMEM((n, 2 * owned, M), F32),
            pltpu.VMEM((n - 1, owned * DH, M), BF16),
            pltpu.VMEM((n - 1, 2 * owned, M), F32),
            pltpu.VMEM((group, M, M), BF16),
            pltpu.VMEM((owned, M, M), F32),
            pltpu.VMEM((M, owned * DH), BF16),
            pltpu.SemaphoreType.DMA((2, n - 1)),
            pltpu.SemaphoreType.DMA((2, n - 1)),
            pltpu.SemaphoreType.DMA((1, copies_of(n))),
            pltpu.SemaphoreType.DMA((1, copies_of(n))),
            pltpu.SemaphoreType.DMA((1,)),
            pltpu.SemaphoreType.DMA,
        ],
        compiler_params=pltpu.CompilerParams(
            collective_id=1, has_side_effects=True, vmem_limit_bytes=VMEM_LIMIT
        ),
        name="landmark_products",
    )(land_q, local_k, keys, values)


def final_kernel(n, own_ref, q_ref, lk_ref, o_ref, held, weights, send_sem, recv_sem, local_sem):
    def weigh(head, carry):
        cols = pl.ds(pl.multiple_of(head * DH, DH), DH)
        scores = dot(q_ref[:, cols], lk_ref[:, cols], NT) * SCALE
        expo = jnp.exp(scores - jnp.max(scores, 1, keepdims=True))
        weights[head] = (expo / jnp.sum(expo, 1, keepdims=True)).astype(BF16)
        return carry

    pieces = hops(n)[1] + 2
    at = 0
    for piece, _ in enumerate(gather_stages(n, [own_ref], [held], send_sem, recv_sem, local_sem)):
        until = H * (piece + 1) // pieces
        lax.fori_loop(at, until, weigh, 0)
        at = until

    def attend(head, carry):
        cols = pl.ds(pl.multiple_of(head * DH, DH), DH)
        rows = pl.ds(pl.multiple_of(head * M, M), M)
        o_ref[:, cols] = dot(weights[head], held[rows, :], NN).astype(BF16)
        return carry

    lax.fori_loop(0, H, attend, 0)


def final(own_product, queries, land_k, n):
    tokens, width = queries.shape
    total = copies_of(n)
    return pl.pallas_call(
        functools.partial(final_kernel, n),
        in_specs=[pl.BlockSpec(memory_space=pltpu.VMEM)] * 3,
        out_specs=pl.BlockSpec(memory_space=pltpu.VMEM),
        out_shape=jax.ShapeDtypeStruct((tokens, width), BF16),
        scratch_shapes=[
            pltpu.VMEM((H * M, DH), BF16),
            pltpu.VMEM((H, tokens, M), BF16),
            pltpu.SemaphoreType.DMA((1, total)),
            pltpu.SemaphoreType.DMA((1, total)),
            pltpu.SemaphoreType.DMA((1,)),
        ],
        compiler_params=pltpu.CompilerParams(
            collective_id=2, has_side_effects=True, vmem_limit_bytes=VMEM_LIMIT
        ),
        name="final",
    )(own_product, queries, land_k)


def body(queries, keys, values):
    devices = lax.axis_size("seq")
    per_device = M // devices
    local_q = means(queries, per_device)
    local_k = means(keys, per_device)
    (land_q,) = gather((local_q,), devices, 0)
    own_product, land_k = landmark_products(land_q, local_k, keys, values, devices)
    return final(own_product.reshape(-1, DH), queries, land_k, devices)


def solution(mesh):
    placed = (P(("doc", "seq"), None),) * 3
    return jax.shard_map(
        body, mesh=mesh, in_specs=placed, out_specs=P(("doc", "seq"), None), check_vma=False
    )
```
